256 devices in a mesh: tm: 4 (over z_lo, core), firm: 64 (over y, x, z_hi).
Axes of the slice: x: 4, y: 4, z: 8 (z_hi: 4, z_lo: 2; z = z_hi * 2 + z_lo), core: 2. Of those that a mesh axis runs over, the one named last changes fastest.
Arguments:
- features: bfloat16 [32, 16384, 256], P('tm', 'firm'), may hold values from -6 to 6
- supply_counts: int32 [32, 16384, 3, 256], P('tm', 'firm'), may hold values from 0 to 3
- bank_ids: int32 [32, 16384], P('tm', 'firm'), may hold values from 0 to 511
- sector_ids: int32 [32, 16384], P('tm', 'firm'), may hold values from 0 to 255
- bank_table: bfloat16 [512, 256], P('firm'), may hold values from -6 to 6
- sector_table: bfloat16 [256, 256], P('firm'), may hold values from -6 to 6
- w_supply: bfloat16 [256, 256], replicated, may hold values from -0.375 to 0.375
- w_query: bfloat16 [256, 256], replicated, may hold values from -0.375 to 0.375
- w_key: bfloat16 [256, 256], replicated, may hold values from -0.375 to 0.375
- w_value: bfloat16 [256, 256], replicated, may hold values from -0.375 to 0.375
- w_out: bfloat16 [256, 256], replicated, may hold values from -0.375 to 0.375
- w_in: bfloat16 [256, 1024], replicated, may hold values from -0.375 to 0.375
- w_down: bfloat16 [1024, 256], replicated, may hold values from -0.1875 to 0.1875
- gain_mix: float32 [256], replicated, may hold values from 0.1 to 1.9
- gain_ffn: float32 [256], replicated, may hold values from 0.1 to 1.9
Outputs:
- result: bfloat16 [32, 16384, 256], P('tm', 'firm')
The draws below stay inside these ranges and needn't reach their ends.
All inputs are finite; a program needn't handle non-finite values.
Results may differ from the reference program's by a relative error of at most 0.0059.
Values may be sent and summed in bfloat16 or wider, within the bound.
No kernel may reach another device: no remote copies, remote signals or barrier semaphores. Data moves between devices by JAX's collectives and lax.ppermute only.
A program may use at most 64 MiB of HBM per device.

```python
import jax
import jax.numpy as jnp
from jax import lax

D = 256
HEADS = 4
HEAD_DIM = 64
FFN = 1024
FIRM_DEV = 256
MONTHS = 32
FIRMS = 16384
BANKS = 512
SECTORS = 256
N_FIRM = 64


def place_ends(entries, own_key, least, top_value):
    extent = entries.shape
    index_at = [jax.random.randint(jax.random.fold_in(own_key, axis), (), 0, extent[axis]) for axis in range(len(extent))]
    entries = entries.at[tuple(index_at)].set(least)
    longest = extent.index(max(extent))
    index_at[longest] = (index_at[longest] + 1) % extent[longest]
    return entries.at[tuple(index_at)].set(top_value)


def block_scale(rng, dims, split, least, largest):
    def one(dim, blocks):
        steps = jax.random.uniform(jax.random.fold_in(jax.random.fold_in(rng, 6), dim), (blocks,), jnp.float32, least / len(split), largest / len(split))
        return jnp.repeat(jnp.exp(steps), dims[dim] // blocks).reshape((-1,) + (1,) * (len(dims) - dim - 1))

    level = one(*split[0])
    for cut in split[1:]:
        level = level * one(*cut)
    return level


def gaussian(key, dims, spread, reach, cuts=(), held_as=jnp.bfloat16):
    factor_of = block_scale(key, dims, cuts, -0.22, 0.18) if cuts else 1.0
    entries = jax.random.normal(key, dims, jnp.float32) * spread * factor_of
    return jnp.minimum(jnp.maximum(entries, -reach), reach).astype(held_as)


def setup_inputs(seed: int = 0) -> dict:
    key_list = jax.random.split(jax.random.key(seed), 16)
    return {
        "features": gaussian(key_list[0], (MONTHS, FIRMS, D), 1.0, 6.0, ((0, 4), (1, 64))),
        "supply_counts": place_ends(jax.random.randint(key_list[1], (MONTHS, FIRMS, 3, FIRM_DEV), 0, 4), jax.random.fold_in(key_list[1], 1), 0, 3).astype(jnp.int32),
        "bank_ids": place_ends(jax.random.randint(key_list[2], (MONTHS, FIRMS), 0, BANKS), jax.random.fold_in(key_list[2], 1), 0, BANKS - 1).astype(jnp.int32),
        "sector_ids": place_ends(jax.random.randint(key_list[3], (MONTHS, FIRMS), 0, SECTORS), jax.random.fold_in(key_list[3], 1), 0, SECTORS - 1).astype(jnp.int32),
        "bank_table": gaussian(key_list[4], (BANKS, D), 1.0, 6.0, ((0, 64),)),
        "sector_table": gaussian(key_list[5], (SECTORS, D), 1.0, 6.0, ((0, 64),)),
        "w_supply": gaussian(key_list[6], (D, D), D ** -0.5, 0.375),
        "w_query": gaussian(key_list[7], (D, D), D ** -0.5, 0.375),
        "w_key": gaussian(key_list[8], (D, D), D ** -0.5, 0.375),
        "w_value": gaussian(key_list[9], (D, D), D ** -0.5, 0.375),
        "w_out": gaussian(key_list[10], (D, D), D ** -0.5, 0.375),
        "w_in": gaussian(key_list[11], (D, FFN), D ** -0.5, 0.375),
        "w_down": gaussian(key_list[12], (FFN, D), FFN ** -0.5, 0.1875),
        "gain_mix": jnp.clip(1.0 + 0.18 * jax.random.normal(key_list[13], (D,), jnp.float32), 0.1, 1.9),
        "gain_ffn": jnp.clip(1.0 + 0.18 * jax.random.normal(key_list[14], (D,), jnp.float32), 0.1, 1.9),
    }


def rms_norm(values, gain):
    scale = lax.rsqrt(lax.optimization_barrier(jnp.mean(values * values, axis=-1, keepdims=True)) + 1e-06)
    return values * scale * gain.astype(jnp.float32)

def reference(features, supply_counts, bank_ids, sector_ids, bank_table, sector_table, w_supply, w_query, w_key, w_value, w_out, w_in, w_down, gain_mix, gain_ffn):

    def month_step(item):
        feats, counts, banks, sectors = item
        supplied = jnp.dot(feats, w_supply, preferred_element_type=jnp.float32).astype(jnp.bfloat16)
        blocks = supplied.reshape(N_FIRM, FIRM_DEV, D)
        padded = jnp.pad(blocks, ((1, 1), (0, 0), (0, 0)))
        window = jnp.concatenate([padded[0:N_FIRM], padded[1:N_FIRM + 1], padded[2:N_FIRM + 2]], axis=1)
        tiles = counts.reshape(N_FIRM, FIRM_DEV, 3 * FIRM_DEV).astype(jnp.float32)
        message = jnp.einsum('pfs,psd->pfd', tiles, window.astype(jnp.float32)).reshape(FIRMS, D)
        degree = 1.0 + lax.optimization_barrier(jnp.sum(counts, axis=(1, 2))).astype(jnp.float32)
        message = message / jnp.sqrt(degree)[:, None]
        hub = bank_table[banks].astype(jnp.float32) + sector_table[sectors].astype(jnp.float32)
        mixed = feats.astype(jnp.float32) + message + hub
        normed = rms_norm(mixed, gain_mix).astype(jnp.bfloat16)
        query = jnp.dot(normed, w_query, preferred_element_type=jnp.float32).astype(jnp.bfloat16)
        key = jnp.dot(normed, w_key, preferred_element_type=jnp.float32).astype(jnp.bfloat16)
        value = jnp.dot(normed, w_value, preferred_element_type=jnp.float32).astype(jnp.bfloat16)
        return (mixed, query, key, value)
    mixed, query, key, value = lax.map(month_step, (features, supply_counts, bank_ids, sector_ids))

    def by_block(array):
        return jnp.swapaxes(array.reshape(MONTHS, N_FIRM, FIRM_DEV, D), 0, 1)

    def block_step(item):
        mixed_b, query_b, key_b, value_b = item
        query4 = query_b.reshape(MONTHS, FIRM_DEV, HEADS, HEAD_DIM).astype(jnp.float32)
        key_pad = jnp.pad(key_b, ((3, 0), (0, 0), (0, 0)))
        value_pad = jnp.pad(value_b, ((3, 0), (0, 0), (0, 0)))
        months_idx = jnp.arange(MONTHS, dtype=jnp.int32)
        total = jnp.zeros((MONTHS, FIRM_DEV, HEADS, HEAD_DIM), jnp.float32)
        for lag in range(4):
            key_l = key_pad[3 - lag:3 - lag + MONTHS].reshape(MONTHS, FIRM_DEV, HEADS, HEAD_DIM).astype(jnp.float32)
            value_l = value_pad[3 - lag:3 - lag + MONTHS].reshape(MONTHS, FIRM_DEV, HEADS, HEAD_DIM).astype(jnp.float32)
            score = jnp.einsum('mfhd,mfhd->mfh', query4, key_l) / jnp.sqrt(jnp.float32(HEAD_DIM)) - jnp.log(jnp.float32(4.0))
            valid = (months_idx - lag >= 0).astype(jnp.float32)[:, None, None]
            total = total + (jax.nn.sigmoid(score) * valid)[..., None] * value_l
        attended = total.astype(jnp.bfloat16).reshape(MONTHS * FIRM_DEV, D)
        second = mixed_b.reshape(MONTHS * FIRM_DEV, D) + jnp.dot(attended, w_out, preferred_element_type=jnp.float32)
        normed2 = rms_norm(second, gain_ffn).astype(jnp.bfloat16)
        inner = jax.nn.gelu(jnp.dot(normed2, w_in, preferred_element_type=jnp.float32)).astype(jnp.bfloat16)
        final = second + jnp.dot(inner, w_down, preferred_element_type=jnp.float32)
        return final.astype(jnp.bfloat16).reshape(MONTHS, FIRM_DEV, D)
    blocks_out = lax.map(block_step, (by_block(mixed), by_block(query), by_block(key), by_block(value)))
    return jnp.swapaxes(blocks_out, 0, 1).reshape(MONTHS, FIRMS, D)
```

```python
import jax
import jax.numpy as jnp
from jax import lax
from jax.experimental import pallas as pl
from jax.experimental.pallas import tpu as pltpu
from jax.sharding import PartitionSpec as P
import math

HEADS = 4
LAGS = 3
EARLY = 5
SLOT = 16
LOG2 = math.log(2.0)
GELU = math.sqrt(2.0 / math.pi)
BF = jnp.bfloat16
F32 = jnp.float32


def mm(a, b):
    return jnp.dot(a, b, preferred_element_type=F32)


def rms_norm(values, gain):
    scale = lax.rsqrt(jnp.mean(values * values, axis=-1, keepdims=True) + 1e-06)
    return values * scale * gain


def mix_month(counts, own, before, after, bank_pos, sector_pos, table, w_supply, gain_mix):
    firms = own.shape[0]
    tiles = [counts[k].astype(F32) for k in range(3)]
    degree = 1.0 + jnp.sum(tiles[0] + tiles[1] + tiles[2], axis=-1, keepdims=True)
    message = jnp.zeros(own.shape, F32)
    for tile, block in zip(tiles, (before, own, after)):
        supplied = mm(block, w_supply).astype(BF)
        message = message + mm(tile.astype(BF), supplied)
    rows = lax.broadcasted_iota(jnp.int32, (table.shape[0], firms), 0)
    chosen = jnp.where((rows == bank_pos) | (rows == sector_pos), 1.0, 0.0).astype(BF)
    hubs = lax.dot_general(chosen, table, (((0,), (0,)), ((), ())), preferred_element_type=F32)
    mixed = own.astype(F32) + message * lax.rsqrt(degree) + hubs
    return mixed, rms_norm(mixed, gain_mix).astype(BF)


def attend(query, keys, values, head_sum):
    total = jnp.zeros(query.shape, F32)
    for key, value in zip(keys, values):
        half = mm(query * key, head_sum) - LOG2
        total = total + (0.5 + 0.5 * jnp.tanh(half)) * value.astype(F32)
    return total.astype(BF)


def finish_month(mixed, attended, w_out, w_in, w_down, gain_ffn):
    second = mixed + mm(attended, w_out)
    normed2 = rms_norm(second, gain_ffn).astype(BF)
    x = mm(normed2, w_in)
    inner = (0.5 * x * (1.0 + jnp.tanh(GELU * (x + 0.044715 * (x * x * x))))).astype(BF)
    return (second + mm(inner, w_down)).astype(BF)


def head_matrix(width):
    size = width // HEADS
    row = lax.broadcasted_iota(jnp.int32, (width, width), 0) // size
    col = lax.broadcasted_iota(jnp.int32, (width, width), 1) // size
    return jnp.where(row == col, 0.5 / math.sqrt(size), 0.0).astype(BF)


def late_kernel(counts, own, before, after, pos, table, w_supply, gain_mix, mixed_out, normed_out):
    mixed, normed = mix_month(
        counts, own[...], before[...], after[...], pos[0:1], pos[1:2], table[...], w_supply[...], gain_mix[...]
    )
    mixed_out[...] = mixed
    normed_out[...] = normed


def early_kernel(
    counts, own, before, after, pos, table, w_supply, gain_mix,
    late_mixed, late_normed, w_qkv, head_sum, w_out, w_in, w_down, gain_ffn,
    result, mixed_out, normed_out, mixed_now, normed_now, ring,
):
    month = pl.program_id(0)
    width = own.shape[-1]

    @pl.when(month < EARLY)
    def _():
        mixed, normed = mix_month(
            counts, own[...], before[...], after[...], pos[0:1], pos[1:2], table[...], w_supply[...], gain_mix[...]
        )
        mixed_now[...] = mixed
        normed_now[...] = normed

    @pl.when(month >= EARLY)
    def _():
        mixed_now[...] = late_mixed[...]
        normed_now[...] = late_normed[...]

    @pl.when(month < LAGS)
    def _():
        mixed_out[...] = mixed_now[...]
        normed_out[...] = normed_now[...]
        ring[lax.rem(month, 4)] = mm(normed_now[...], w_qkv[:, width:]).astype(BF)

    @pl.when(month >= LAGS)
    def _():
        qkv = mm(normed_now[...], w_qkv[...]).astype(BF)
        ring[lax.rem(month, 4)] = qkv[:, width:]
        slots = [lax.rem(month + 4 - lag, 4) for lag in range(LAGS + 1)]
        attended = attend(
            qkv[:, :width], [ring[s, :, :width] for s in slots], [ring[s, :, width:] for s in slots], head_sum[...]
        )
        result[...] = finish_month(mixed_now[...], attended, w_out[...], w_in[...], w_down[...], gain_ffn[...])


def first_kernel(
    mixed, normed, earlier, w_qkv, head_sum, w_out, w_in, w_down, gain_ffn, started, result, ring,
):
    del started
    month = pl.program_id(0)
    width = normed.shape[-1]

    @pl.when(month == 0)
    def _():
        for i in range(LAGS):
            ring[i + 1] = mm(earlier[i], w_qkv[:, width:]).astype(BF)

    qkv = mm(normed[...], w_qkv[...]).astype(BF)
    ring[lax.rem(month, 4)] = qkv[:, width:]
    slots = [lax.rem(month + 4 - lag, 4) for lag in range(LAGS + 1)]
    attended = attend(
        qkv[:, :width], [ring[s, :, :width] for s in slots], [ring[s, :, width:] for s in slots], head_sum[...]
    )
    result[...] = finish_month(mixed[...], attended, w_out[...], w_in[...], w_down[...], gain_ffn[...])


def month_spec(shape, index):
    return pl.BlockSpec((None,) + shape, lambda m: (index(m),) + (0,) * len(shape))


def whole(*shape):
    return pl.BlockSpec(shape, lambda m: (0,) * len(shape))


def body(
    features, supply_counts, bank_ids, sector_ids, bank_table, sector_table,
    w_supply, w_query, w_key, w_value, w_out, w_in, w_down, gain_mix, gain_ffn,
):
    months, firms, width = features.shape
    inner = w_in.shape[1]
    devices = lax.axis_size("firm")
    me = lax.axis_index("firm")
    up = [(i, i + 1) for i in range(devices - 1)]
    down = [(j, i) for i, j in up]
    late_count = months - EARLY

    def swap(x, bits):
        return lax.ppermute(x, "firm", [(i, i ^ bits) for i in range(devices)])

    late = features[EARLY:]
    late_before = lax.ppermute(late, "firm", up)
    late_after = lax.ppermute(late, "firm", down)

    bank_local, sector_local = bank_table.shape[0], sector_table.shape[0]
    hub = jnp.concatenate(
        [bank_table, sector_table, jnp.zeros((SLOT - bank_local - sector_local, width), BF)], axis=0
    )
    hub = jnp.concatenate([hub, swap(hub, 1), swap(hub, 2), swap(hub, 3)], axis=0)

    early = features[:EARLY]
    early_before = lax.ppermute(early, "firm", up)
    early_after = lax.ppermute(early, "firm", down)

    for stage in (4, 8, 16, 32):
        hub = jnp.concatenate([hub, swap(hub, stage)], axis=0)

    bank_pos = ((bank_ids // bank_local) ^ me) * SLOT + bank_ids % bank_local
    sector_pos = ((sector_ids // sector_local) ^ me) * SLOT + bank_local + sector_ids % sector_local
    pos = jnp.stack([bank_pos, sector_pos], axis=1)

    counts = jnp.transpose(supply_counts, (0, 2, 1, 3))
    gain_mix = gain_mix.reshape(1, width)
    gain_ffn = gain_ffn.reshape(1, width)
    w_qkv = jnp.concatenate([w_query, w_key, w_value], axis=1)
    head_sum = head_matrix(width)
    hub_rows = hub.shape[0]

    mix_flops = 2 * firms * width * (3 * width + 3 * firms + hub_rows)
    end_flops = 2 * firms * width * (8 * width + 2 * inner)

    def cost(mixes, ends):
        return pl.CostEstimate(
            flops=mixes * mix_flops + ends * end_flops,
            bytes_accessed=mixes * firms * width * 24 + ends * firms * width * 10,
            transcendentals=ends * firms * (inner + 4 * width),
        )

    f32_month = (firms, width)
    late_mixed, late_normed = pl.pallas_call(
        late_kernel,
        grid=(late_count,),
        in_specs=[
            month_spec((3, firms, firms), lambda m: m + EARLY),
            month_spec(f32_month, lambda m: m + EARLY),
            month_spec(f32_month, lambda m: m),
            month_spec(f32_month, lambda m: m),
            month_spec((2, firms), lambda m: m + EARLY),
            whole(hub_rows, width),
            whole(width, width),
            whole(1, width),
        ],
        out_specs=[month_spec(f32_month, lambda m: m)] * 2,
        out_shape=[
            jax.ShapeDtypeStruct((late_count, firms, width), F32),
            jax.ShapeDtypeStruct((late_count, firms, width), BF),
        ],
        cost_estimate=cost(late_count, 0),
        name="late_mix",
    )(counts, features, late_before, late_after, pos, hub, w_supply, gain_mix)

    earlier = lax.ppermute(late_normed, "tm", [(i, i + 1) for i in range(lax.axis_size("tm") - 1)])

    clamp = lambda m: jnp.minimum(m, EARLY - 1)
    tail = lambda m: jnp.maximum(m - EARLY, 0)
    first = lambda m: jnp.minimum(m, LAGS - 1)
    weights = (w_qkv, head_sum, w_out, w_in, w_down, gain_ffn)
    weight_specs = [
        whole(width, 3 * width), whole(width, width), whole(width, width),
        whole(width, inner), whole(inner, width), whole(1, width),
    ]
    started, first_mixed, first_normed = pl.pallas_call(
        early_kernel,
        grid=(months,),
        in_specs=[
            month_spec((3, firms, firms), clamp),
            month_spec(f32_month, clamp),
            month_spec(f32_month, clamp),
            month_spec(f32_month, clamp),
            month_spec((2, firms), clamp),
            whole(hub_rows, width),
            whole(width, width),
            whole(1, width),
            month_spec(f32_month, tail),
            month_spec(f32_month, tail),
        ] + weight_specs,
        out_specs=[
            month_spec(f32_month, lambda m: jnp.maximum(m, LAGS)),
            month_spec(f32_month, first),
            month_spec(f32_month, first),
        ],
        out_shape=[
            jax.ShapeDtypeStruct((months, firms, width), BF),
            jax.ShapeDtypeStruct((LAGS, firms, width), F32),
            jax.ShapeDtypeStruct((LAGS, firms, width), BF),
        ],
        scratch_shapes=[
            pltpu.VMEM((firms, width), F32),
            pltpu.VMEM((firms, width), BF),
            pltpu.VMEM((4, firms, 2 * width), BF),
        ],
        cost_estimate=cost(EARLY, months - LAGS),
        name="early_mix_and_finish",
    )(counts, features, early_before, early_after, pos, hub, w_supply, gain_mix, late_mixed, late_normed, *weights)

    return pl.pallas_call(
        first_kernel,
        grid=(LAGS,),
        in_specs=[
            month_spec(f32_month, lambda m: m),
            month_spec(f32_month, lambda m: m),
            whole(LAGS, firms, width),
        ] + weight_specs + [pl.BlockSpec(memory_space=pl.ANY)],
        out_specs=month_spec(f32_month, lambda m: m),
        out_shape=jax.ShapeDtypeStruct((months, firms, width), BF),
        scratch_shapes=[pltpu.VMEM((4, firms, 2 * width), BF)],
        input_output_aliases={9: 0},
        cost_estimate=cost(0, LAGS),
        name="first_finish",
    )(first_mixed, first_normed, earlier, *weights, started)


def solution(mesh):
    in_specs = (
        P("tm", "firm", None),
        P("tm", "firm", None, None),
        P("tm", "firm"),
        P("tm", "firm"),
        P("firm", None),
        P("firm", None),
    ) + (P(),) * 9
    return jax.shard_map(body, mesh=mesh, in_specs=in_specs, out_specs=P("tm", "firm", None), check_vma=False)
```

```python
import math

import jax
import jax.numpy as jnp
from jax import lax
from jax.experimental import pallas as pl
from jax.experimental.pallas import tpu as pltpu
from jax.sharding import PartitionSpec as P

HEADS = 4
LAGS = 3
HALF = 4
SLOT = 16
LOG2 = math.log(2.0)
GELU = math.sqrt(2.0 / math.pi)
BF = jnp.bfloat16
F32 = jnp.float32
VM = pl.BlockSpec(memory_space=pltpu.VMEM)
SM = pl.BlockSpec(memory_space=pltpu.SMEM)
ANY = pl.BlockSpec(memory_space=pl.ANY)


def mm(a, b):
    return jnp.dot(a, b, preferred_element_type=F32)


def rms_norm(values, gain):
    scale = lax.rsqrt(jnp.mean(values * values, axis=-1, keepdims=True) + 1e-06)
    return values * scale * gain


def head_matrix(width):
    size = width // HEADS
    row = lax.broadcasted_iota(jnp.int32, (width, width), 0) // size
    col = lax.broadcasted_iota(jnp.int32, (width, width), 1) // size
    return jnp.where(row == col, 0.5 / math.sqrt(size), 0.0).astype(BF)


def attend(query, keys, values, head_sum):
    total = jnp.zeros(query.shape, F32)
    for key, value in zip(keys, values):
        value = value.astype(F32)
        total = total + (value + jnp.tanh(mm(query * key, head_sum) - LOG2) * value)
    return (0.5 * total).astype(BF)


def finish(mixed, attended, w_out, w_in, w_down, gain_ffn):
    second = mixed + mm(attended, w_out)
    normed2 = rms_norm(second, gain_ffn).astype(BF)
    x = mm(normed2, w_in)
    half = 0.5 * x
    inner = (half + half * jnp.tanh(x * (GELU + (GELU * 0.044715) * (x * x)))).astype(BF)
    return (second + mm(inner, w_down)).astype(BF)


def stack(parts):
    return jnp.concatenate(parts, axis=0)


def lagged(parts, count):
    return [stack(parts[LAGS - lag : LAGS - lag + count]) for lag in range(LAGS + 1)]


def own_kernel(where, counts, own, w_supply, base, tiles, scale):
    even = 2 - 2 * where[1]
    odd = 2 * where[1]
    for m in range(own.shape[0]):
        part = [counts[m, k].astype(F32) for k in range(3)]
        degree = 1.0 + jnp.sum(part[0] + part[1] + part[2], axis=-1, keepdims=True)
        inverse = lax.rsqrt(degree)
        feats = own[m]
        supplied = mm(feats, w_supply[...]).astype(BF)
        base[m] = feats.astype(F32) + inverse * mm(part[1].astype(BF), supplied)
        scale[m] = jnp.broadcast_to(inverse, scale.shape[1:])
        tiles[m, 0] = counts[m, even].astype(F32).astype(BF)
        tiles[m, 1] = counts[m, odd].astype(F32).astype(BF)


def mix(m, base, tiles, scale, even_rows, odd_rows, w_supply):
    message = mm(tiles[m, 0], mm(even_rows, w_supply).astype(BF))
    message = message + mm(tiles[m, 1], mm(odd_rows, w_supply).astype(BF))
    spread = jnp.concatenate([scale[m]] * (base.shape[-1] // scale.shape[-1]), axis=-1)
    return base + spread * message


def late_kernel(
    where, base, tiles, scale, even_rows, odd_rows, banks, sectors, *rest,
):
    tables, (w_supply, w_query, w_key, w_value, gain_mix) = rest[:4], rest[4:9]
    early_base, mixed_out, normed_out, query_out, key_out, value_out = rest[9:]
    me = where[0]
    rows_each, firms = tables[0].shape[0], base.shape[1]
    row = lax.broadcasted_iota(jnp.int32, (rows_each, firms), 0)
    normed = []
    for m in list(range(HALF, 2 * HALF)) + list(range(HALF)):
        bank, sector = banks[m : m + 1], sectors[m : m + 1]
        bank = (lax.shift_right_logical(bank, 3) ^ me) * SLOT + (bank & 7)
        sector = (lax.shift_right_logical(sector, 2) ^ me) * SLOT + 8 + (sector & 3)
        total = base[m]
        for i, table in enumerate(tables):
            chosen = jnp.where((row == bank - i * rows_each) | (row == sector - i * rows_each), 1.0, 0.0)
            total = total + lax.dot_general(
                chosen.astype(BF), table[...], (((0,), (0,)), ((), ())), preferred_element_type=F32
            )
        if m < HALF:
            early_base[m] = total
        else:
            mixed = mix(m, total, tiles, scale, even_rows[m - HALF], odd_rows[m - HALF], w_supply[...])
            mixed_out[m - HALF] = mixed
            normed.append(rms_norm(mixed, gain_mix[...]).astype(BF))
            if m >= 2 * HALF - LAGS:
                normed_out[m - 2 * HALF + LAGS] = normed[-1]
    shape = query_out.shape
    rows = stack(normed)
    query_out[...] = mm(rows, w_query[...]).astype(BF).reshape(shape)
    key_out[...] = mm(rows, w_key[...]).astype(BF).reshape(shape)
    value_out[...] = mm(rows, w_value[...]).astype(BF).reshape(shape)


def write_back(final, buffer, result, sems, first):
    firms = buffer.shape[1]
    copies = []
    for i in range(buffer.shape[0]):
        buffer[i] = final[i * firms : (i + 1) * firms]
        copies.append(pltpu.make_async_copy(buffer.at[i], result.at[first + i], sems.at[i]))
        copies[-1].start()
    for copy in copies:
        copy.wait()


def last_kernel(mixed, query, key, value, w_out, w_in, w_down, gain_ffn, result, buffer, sems):
    attended = attend(
        query[LAGS], [key[LAGS - j] for j in range(LAGS + 1)], [value[LAGS - j] for j in range(LAGS + 1)],
        head_matrix(query.shape[-1]),
    )
    final = finish(mixed[LAGS], attended, w_out[...], w_in[...], w_down[...], gain_ffn[...])
    write_back(final, buffer, result, sems, 2 * HALF - 1)


def early_kernel(
    base, tiles, scale, even_rows, odd_rows, late_mixed, late_query, late_key, late_value,
    w_supply, w_query, w_key, w_value, gain_mix, w_out, w_in, w_down, gain_ffn, started,
    result, mixed_out, query_out, key_out, value_out, buffer, sems,
):
    del started
    firms = base.shape[1]
    mixed, normed = [], []
    for m in range(HALF):
        mixed.append(mix(m, base[m], tiles, scale, even_rows[m], odd_rows[m], w_supply[...]))
        normed.append(rms_norm(mixed[-1], gain_mix[...]).astype(BF))
    rows = stack(normed)
    cut = lambda rows: [rows[i * firms : (i + 1) * firms] for i in range(HALF)]
    query = cut(mm(rows, w_query[...]).astype(BF))
    key = cut(mm(rows, w_key[...]).astype(BF))
    value = cut(mm(rows, w_value[...]).astype(BF))
    for m in range(LAGS):
        mixed_out[m], query_out[m], key_out[m], value_out[m] = mixed[m], query[m], key[m], value[m]
    keys = lagged(key + [late_key[m] for m in range(LAGS)], HALF)
    values = lagged(value + [late_value[m] for m in range(LAGS)], HALF)
    queries = stack([query[LAGS]] + [late_query[m] for m in range(LAGS)])
    attended = attend(queries, keys, values, head_matrix(base.shape[-1]))
    total = stack([mixed[LAGS]] + [late_mixed[m] for m in range(LAGS)])
    final = finish(total, attended, w_out[...], w_in[...], w_down[...], gain_ffn[...])
    write_back(final, buffer, result, sems, LAGS)


def first_kernel(
    earlier, mixed, query, key, value, w_key, w_value, w_out, w_in, w_down, gain_ffn, started, result, buffer, sems,
):
    del started
    firms, width = mixed.shape[1:]
    rows = earlier[...].reshape(LAGS * firms, width)
    cut = lambda rows: [rows[i * firms : (i + 1) * firms] for i in range(LAGS)]
    keys = lagged(cut(mm(rows, w_key[...]).astype(BF)) + [key[m] for m in range(LAGS)], LAGS)
    values = lagged(cut(mm(rows, w_value[...]).astype(BF)) + [value[m] for m in range(LAGS)], LAGS)
    flat = (LAGS * firms, width)
    attended = attend(query[...].reshape(flat), keys, values, head_matrix(width))
    final = finish(mixed[...].reshape(flat), attended, w_out[...], w_in[...], w_down[...], gain_ffn[...])
    write_back(final, buffer, result, sems, 0)


def body(
    features, supply_counts, bank_ids, sector_ids, bank_table, sector_table,
    w_supply, w_query, w_key, w_value, w_out, w_in, w_down, gain_mix, gain_ffn,
):
    months, firms, width = features.shape
    inner = w_in.shape[1]
    devices = lax.axis_size("firm")
    me = lax.axis_index("firm")
    where = jnp.stack([me, me & 1]).astype(jnp.int32)
    even_pairs = [(i, i ^ 1) for i in range(devices)]
    odd_pairs = [(i, i + 1) for i in range(1, devices - 1, 2)]
    odd_pairs = odd_pairs + [(j, i) for i, j in odd_pairs]

    def swap(x, bits):
        return lax.ppermute(x, "firm", [(i, i ^ bits) for i in range(devices)])

    late = features[HALF:]
    late_even = lax.ppermute(late, "firm", even_pairs)
    late_odd = lax.ppermute(late, "firm", odd_pairs)

    spare = SLOT - bank_table.shape[0] - sector_table.shape[0]
    hub = jnp.concatenate([bank_table, sector_table, jnp.zeros((spare, width), BF)], axis=0)
    hub, late = lax.optimization_barrier((hub, late))
    hub = jnp.concatenate([hub] + [swap(hub, i) for i in (1, 2, 3)], axis=0)

    early = features[:HALF]
    early_even = lax.ppermute(early, "firm", even_pairs)
    early_odd = lax.ppermute(early, "firm", odd_pairs)

    hub = jnp.concatenate([hub] + [swap(hub, i) for i in (4, 8, 12)], axis=0)
    tables = [hub] + [swap(hub, i) for i in (16, 32, 48)]

    counts = jnp.transpose(supply_counts, (0, 2, 1, 3))
    gain_mix = gain_mix.reshape(1, width)
    gain_ffn = gain_ffn.reshape(1, width)

    def cost(units, mebibytes):
        return pl.CostEstimate(
            flops=2 * units * firms * width * width, bytes_accessed=mebibytes << 20, transcendentals=0
        )

    def like(count, dtype, lanes=width):
        return jax.ShapeDtypeStruct((count, firms, lanes), dtype)

    params = pltpu.CompilerParams(vmem_limit_bytes=28 << 20)
    step = lambda *shape: pl.BlockSpec((2,) + shape, lambda m: (m,) + (0,) * len(shape))
    base, tiles, scale = pl.pallas_call(
        own_kernel,
        grid=(months // 2,),
        in_specs=[
            SM, step(3, firms, firms), step(firms, width), pl.BlockSpec((width, width), lambda m: (0, 0)),
        ],
        out_specs=[step(firms, width), step(2, firms, firms), step(firms, 128)],
        out_shape=[
            like(months, F32), jax.ShapeDtypeStruct((months, 2, firms, firms), BF), like(months, F32, 128),
        ],
        compiler_params=params,
        cost_estimate=cost(16, 12),
        name="own_block",
    )(where, counts, features, w_supply)

    early_base, late_mixed, late_normed, late_query, late_key, late_value = pl.pallas_call(
        late_kernel,
        in_specs=[SM] + [VM] * 16,
        out_specs=[VM] * 6,
        out_shape=[
            like(HALF, F32), like(HALF, F32), like(LAGS, BF), like(HALF, BF), like(HALF, BF), like(HALF, BF),
        ],
        compiler_params=params,
        cost_estimate=cost(60, 12),
        name="late_months",
    )(
        where, base, tiles, scale, late_even, late_odd, bank_ids, sector_ids, *tables,
        w_supply, w_query, w_key, w_value, gain_mix,
    )

    earlier = lax.ppermute(late_normed, "tm", [(i, i + 1) for i in range(lax.axis_size("tm") - 1)])
    end_weights = (w_out, w_in, w_down, gain_ffn)

    def scratch(count):
        return [pltpu.VMEM((count, firms, width), BF), pltpu.SemaphoreType.DMA((count,))]

    result = pl.pallas_call(
        last_kernel,
        in_specs=[VM] * 8,
        out_specs=ANY,
        out_shape=like(months, BF),
        scratch_shapes=scratch(1),
        compiler_params=params,
        cost_estimate=cost(16, 3),
        name="last_month",
    )(late_mixed, late_query, late_key, late_value, *end_weights)

    result, mixed, query, key, value = pl.pallas_call(
        early_kernel,
        in_specs=[VM] * 18 + [ANY],
        out_specs=[ANY] + [VM] * 4,
        out_shape=[like(months, BF), like(LAGS, F32), like(LAGS, BF), like(LAGS, BF), like(LAGS, BF)],
        scratch_shapes=scratch(HALF),
        input_output_aliases={18: 0},
        compiler_params=params,
        cost_estimate=cost(90, 8),
        name="early_months",
    )(
        early_base, tiles, scale, early_even, early_odd, late_mixed, late_query, late_key, late_value,
        w_supply, w_query, w_key, w_value, gain_mix, *end_weights, result,
    )

    return pl.pallas_call(
        first_kernel,
        in_specs=[VM] * 11 + [ANY],
        out_specs=ANY,
        out_shape=like(months, BF),
        scratch_shapes=scratch(LAGS),
        input_output_aliases={11: 0},
        compiler_params=params,
        cost_estimate=cost(54, 4),
        name="first_months",
    )(earlier, mixed, query, key, value, w_key, w_value, *end_weights, result)


def solution(mesh):
    in_specs = (
        P("tm", "firm", None),
        P("tm", "firm", None, None),
        P("tm", "firm"),
        P("tm", "firm"),
        P("firm", None),
        P("firm", None),
    ) + (P(),) * 9
    return jax.shard_map(body, mesh=mesh, in_specs=in_specs, out_specs=P("tm", "firm", None), check_vma=False)
```

```python
import math

import jax
import jax.numpy as jnp
from jax import lax
from jax.experimental import pallas as pl
from jax.experimental.pallas import tpu as pltpu
from jax.sharding import PartitionSpec as P

HEADS = 4
LAGS = 3
HALF = 4
SLOT = 16
LOG2 = math.log(2.0)
GELU = math.sqrt(2.0 / math.pi)
BF = jnp.bfloat16
F32 = jnp.float32
VM = pl.BlockSpec(memory_space=pltpu.VMEM)
SM = pl.BlockSpec(memory_space=pltpu.SMEM)
ANY = pl.BlockSpec(memory_space=pl.ANY)


def mm(a, b):
    return jnp.dot(a, b, preferred_element_type=F32)


def rms_norm(values, gain):
    scale = lax.rsqrt(jnp.mean(values * values, axis=-1, keepdims=True) + 1e-06)
    return values * scale * gain


def head_matrix(width):
    size = width // HEADS
    row = lax.broadcasted_iota(jnp.int32, (width, width), 0) // size
    col = lax.broadcasted_iota(jnp.int32, (width, width), 1) // size
    return jnp.where(row == col, 0.5 / math.sqrt(size), 0.0).astype(BF)


def attend(query, keys, values, head_sum):
    total = jnp.zeros(query.shape, F32)
    for key, value in zip(keys, values):
        value = value.astype(F32)
        total = total + (value + jnp.tanh(mm(query * key, head_sum) - LOG2) * value)
    return (0.5 * total).astype(BF)


def finish(mixed, attended, w_out, w_in, w_down, gain_ffn):
    second = mixed + mm(attended, w_out)
    normed2 = rms_norm(second, gain_ffn).astype(BF)
    x = mm(normed2, w_in)
    half = 0.5 * x
    inner = (half + half * jnp.tanh(x * (GELU + (GELU * 0.044715) * (x * x)))).astype(BF)
    return (second + mm(inner, w_down)).astype(BF)


def stack(parts):
    return jnp.concatenate(parts, axis=0)


def lagged(parts, count):
    return [stack(parts[LAGS - lag : LAGS - lag + count]) for lag in range(LAGS + 1)]


def own_kernel(where, counts, own, w_supply, base, tiles, scale):
    even = 2 - 2 * where[1]
    odd = 2 * where[1]
    for m in range(own.shape[0]):
        part = [counts[m, k].astype(F32) for k in range(3)]
        degree = 1.0 + jnp.sum(part[0] + part[1] + part[2], axis=-1, keepdims=True)
        inverse = lax.rsqrt(degree)
        feats = own[m]
        supplied = mm(feats, w_supply[...]).astype(BF)
        base[m] = feats.astype(F32) + inverse * mm(part[1].astype(BF), supplied)
        scale[m] = jnp.broadcast_to(inverse, scale.shape[1:])
        tiles[m, 0] = counts[m, even].astype(F32).astype(BF)
        tiles[m, 1] = counts[m, odd].astype(F32).astype(BF)


def mix(m, base, tiles, scale, even_rows, odd_rows, w_supply):
    message = mm(tiles[m, 0], mm(even_rows, w_supply).astype(BF))
    message = message + mm(tiles[m, 1], mm(odd_rows, w_supply).astype(BF))
    spread = jnp.concatenate([scale[m]] * (base.shape[-1] // scale.shape[-1]), axis=-1)
    return base + spread * message


def late_kernel(
    where, base, tiles, scale, even_rows, odd_rows, banks, sectors, *rest,
):
    tables, (w_supply, w_query, w_key, w_value, gain_mix) = rest[:4], rest[4:9]
    early_base, mixed_out, normed_out, query_out, key_out, value_out = rest[9:]
    me = where[0]
    rows_each, firms = tables[0].shape[0], base.shape[1]
    row = lax.broadcasted_iota(jnp.int32, (rows_each, firms), 0)
    normed = []
    for m in list(range(HALF, 2 * HALF)) + list(range(HALF)):
        bank, sector = banks[m : m + 1], sectors[m : m + 1]
        bank = (lax.shift_right_logical(bank, 3) ^ me) * SLOT + (bank & 7)
        sector = (lax.shift_right_logical(sector, 2) ^ me) * SLOT + 8 + (sector & 3)
        total = base[m]
        for i, table in enumerate(tables):
            chosen = jnp.where((row == bank - i * rows_each) | (row == sector - i * rows_each), 1.0, 0.0)
            total = total + lax.dot_general(
                chosen.astype(BF), table[...], (((0,), (0,)), ((), ())), preferred_element_type=F32
            )
        if m < HALF:
            early_base[m] = total
        else:
            mixed = mix(m, total, tiles, scale, even_rows[(m - HALF) * firms : (m - HALF + 1) * firms], odd_rows[m - HALF], w_supply[...])
            mixed_out[m - HALF] = mixed
            normed.append(rms_norm(mixed, gain_mix[...]).astype(BF))
            if m >= 2 * HALF - LAGS:
                normed_out[m - 2 * HALF + LAGS] = normed[-1]
    shape = query_out.shape
    rows = stack(normed)
    query_out[...] = mm(rows, w_query[...]).astype(BF).reshape(shape)
    key_out[...] = mm(rows, w_key[...]).astype(BF).reshape(shape)
    value_out[...] = mm(rows, w_value[...]).astype(BF).reshape(shape)


def write_back(final, buffer, result, sems, first):
    firms = buffer.shape[1]
    copies = []
    for i in range(buffer.shape[0]):
        buffer[i] = final[i * firms : (i + 1) * firms]
        copies.append(pltpu.make_async_copy(buffer.at[i], result.at[first + i], sems.at[i]))
        copies[-1].start()
    for copy in copies:
        copy.wait()


def last_kernel(mixed, query, key, value, w_out, w_in, w_down, gain_ffn, result, buffer, sems):
    attended = attend(
        query[LAGS], [key[LAGS - j] for j in range(LAGS + 1)], [value[LAGS - j] for j in range(LAGS + 1)],
        head_matrix(query.shape[-1]),
    )
    final = finish(mixed[LAGS], attended, w_out[...], w_in[...], w_down[...], gain_ffn[...])
    write_back(final, buffer, result, sems, 2 * HALF - 1)


def early_kernel(
    base, tiles, scale, even_rows, odd_rows, late_mixed, late_query, late_key, late_value,
    w_supply, w_query, w_key, w_value, gain_mix, w_out, w_in, w_down, gain_ffn, started,
    result, mixed_out, query_out, key_out, value_out, buffer, sems,
):
    del started
    firms = base.shape[1]
    mixed, normed = [], []
    for m in range(HALF):
        mixed.append(mix(m, base[m], tiles, scale, even_rows[m], odd_rows[m], w_supply[...]))
        normed.append(rms_norm(mixed[-1], gain_mix[...]).astype(BF))
    rows = stack(normed)
    cut = lambda rows: [rows[i * firms : (i + 1) * firms] for i in range(HALF)]
    query = cut(mm(rows, w_query[...]).astype(BF))
    key = cut(mm(rows, w_key[...]).astype(BF))
    value = cut(mm(rows, w_value[...]).astype(BF))
    for m in range(LAGS):
        mixed_out[m], query_out[m], key_out[m], value_out[m] = mixed[m], query[m], key[m], value[m]
    keys = lagged(key + [late_key[m] for m in range(LAGS)], HALF)
    values = lagged(value + [late_value[m] for m in range(LAGS)], HALF)
    queries = stack([query[LAGS]] + [late_query[m] for m in range(LAGS)])
    attended = attend(queries, keys, values, head_matrix(base.shape[-1]))
    total = stack([mixed[LAGS]] + [late_mixed[m] for m in range(LAGS)])
    final = finish(total, attended, w_out[...], w_in[...], w_down[...], gain_ffn[...])
    write_back(final, buffer, result, sems, LAGS)


def first_kernel(
    earlier, mixed, query, key, value, w_key, w_value, w_out, w_in, w_down, gain_ffn, started, result, buffer, sems,
):
    del started
    firms, width = mixed.shape[1:]
    rows = earlier[...].reshape(LAGS * firms, width)
    cut = lambda rows: [rows[i * firms : (i + 1) * firms] for i in range(LAGS)]
    keys = lagged(cut(mm(rows, w_key[...]).astype(BF)) + [key[m] for m in range(LAGS)], LAGS)
    values = lagged(cut(mm(rows, w_value[...]).astype(BF)) + [value[m] for m in range(LAGS)], LAGS)
    flat = (LAGS * firms, width)
    attended = attend(query[...].reshape(flat), keys, values, head_matrix(width))
    final = finish(mixed[...].reshape(flat), attended, w_out[...], w_in[...], w_down[...], gain_ffn[...])
    write_back(final, buffer, result, sems, 0)


def body(
    features, supply_counts, bank_ids, sector_ids, bank_table, sector_table,
    w_supply, w_query, w_key, w_value, w_out, w_in, w_down, gain_mix, gain_ffn,
):
    months, firms, width = features.shape
    inner = w_in.shape[1]
    devices = lax.axis_size("firm")
    me = lax.axis_index("firm")
    where = jnp.stack([me, me & 1]).astype(jnp.int32)
    even_pairs = [(i, i ^ 1) for i in range(devices)]
    odd_pairs = [(i, i + 1) for i in range(1, devices - 1, 2)]
    odd_pairs = odd_pairs + [(j, i) for i, j in odd_pairs]

    def swap(x, bits):
        return lax.ppermute(x, "firm", [(i, i ^ bits) for i in range(devices)])

    spare = SLOT - bank_table.shape[0] - sector_table.shape[0]
    hub = jnp.concatenate([bank_table, sector_table, jnp.zeros((spare, width), BF)], axis=0)
    across = swap(hub, 2)
    late = features[HALF:]
    plain = late.reshape(HALF * firms, width)
    loaded = jnp.concatenate([plain, hub, jnp.zeros((SLOT, width), BF)], axis=0)
    loaded, late, across = lax.optimization_barrier((loaded, late, across))
    loaded = lax.dynamic_update_slice(loaded, across, (HALF * firms + SLOT, 0))
    late_even = lax.ppermute(loaded, "firm", even_pairs)
    late_odd = lax.ppermute(late, "firm", odd_pairs)

    counts = jnp.transpose(supply_counts, (0, 2, 1, 3))
    gain_mix = gain_mix.reshape(1, width)
    gain_ffn = gain_ffn.reshape(1, width)

    def cost(units, kibibytes):
        return pl.CostEstimate(
            flops=2 * units * firms * width * width, bytes_accessed=kibibytes << 10, transcendentals=0
        )

    def like(count, dtype, lanes=width):
        return jax.ShapeDtypeStruct((count, firms, lanes), dtype)

    params = pltpu.CompilerParams(vmem_limit_bytes=28 << 20)
    step = lambda *shape: pl.BlockSpec((2,) + shape, lambda m: (m,) + (0,) * len(shape))
    base, tiles, scale = pl.pallas_call(
        own_kernel,
        grid=(months // 2,),
        in_specs=[
            SM, step(3, firms, firms), step(firms, width), pl.BlockSpec((width, width), lambda m: (0, 0)),
        ],
        out_specs=[step(firms, width), step(2, firms, firms), step(firms, 128)],
        out_shape=[
            like(months, F32), jax.ShapeDtypeStruct((months, 2, firms, firms), BF), like(months, F32, 128),
        ],
        compiler_params=params,
        cost_estimate=cost(16, 1 << 16),
        name="own_block",
    )(where, counts, features, w_supply)

    base, early = lax.optimization_barrier((base, features[:HALF]))
    early_even = lax.ppermute(early, "firm", even_pairs)
    early_odd = lax.ppermute(early, "firm", odd_pairs)

    def spread(near):
        hub = jnp.concatenate(near, axis=0)
        hub = jnp.concatenate([hub] + [swap(hub, i) for i in (4, 8, 12)], axis=0)
        return [hub] + [swap(hub, i) for i in (16, 32, 48)]

    late_even, late_odd = lax.optimization_barrier((late_even, late_odd))
    arrived = late_even[HALF * firms :]
    near = [hub, arrived[:SLOT], across, arrived[SLOT:]]
    plane = jax.ShapeDtypeStruct((SLOT * 16, width), BF)
    tables = lax.cond(
        me >= 0, spread, lambda near: [jnp.zeros(plane.shape, BF)] * 4, near
    )

    early_base, late_mixed, late_normed, late_query, late_key, late_value = pl.pallas_call(
        late_kernel,
        in_specs=[SM] + [VM] * 16,
        out_specs=[VM] * 6,
        out_shape=[
            like(HALF, F32), like(HALF, F32), like(LAGS, BF), like(HALF, BF), like(HALF, BF), like(HALF, BF),
        ],
        compiler_params=params,
        cost_estimate=cost(1, 1),
        name="late_months",
    )(
        where, base, tiles, scale, late_even, late_odd, bank_ids, sector_ids, *tables,
        w_supply, w_query, w_key, w_value, gain_mix,
    )

    earlier = lax.ppermute(late_normed, "tm", [(i, i + 1) for i in range(lax.axis_size("tm") - 1)])
    end_weights = (w_out, w_in, w_down, gain_ffn)

    def scratch(count):
        return [pltpu.VMEM((count, firms, width), BF), pltpu.SemaphoreType.DMA((count,))]

    result = pl.pallas_call(
        last_kernel,
        in_specs=[VM] * 8,
        out_specs=ANY,
        out_shape=like(months, BF),
        scratch_shapes=scratch(1),
        compiler_params=params,
        cost_estimate=cost(1, 1),
        name="last_month",
    )(late_mixed, late_query, late_key, late_value, *end_weights)

    result, mixed, query, key, value = pl.pallas_call(
        early_kernel,
        in_specs=[VM] * 18 + [ANY],
        out_specs=[ANY] + [VM] * 4,
        out_shape=[like(months, BF), like(LAGS, F32), like(LAGS, BF), like(LAGS, BF), like(LAGS, BF)],
        scratch_shapes=scratch(HALF),
        input_output_aliases={18: 0},
        compiler_params=params,
        cost_estimate=cost(1, 1),
        name="early_months",
    )(
        early_base, tiles, scale, early_even, early_odd, late_mixed, late_query, late_key, late_value,
        w_supply, w_query, w_key, w_value, gain_mix, *end_weights, result,
    )

    return pl.pallas_call(
        first_kernel,
        in_specs=[VM] * 11 + [ANY],
        out_specs=ANY,
        out_shape=like(months, BF),
        scratch_shapes=scratch(LAGS),
        input_output_aliases={11: 0},
        compiler_params=params,
        cost_estimate=cost(1, 1),
        name="first_months",
    )(earlier, mixed, query, key, value, w_key, w_value, *end_weights, result)


def solution(mesh):
    in_specs = (
        P("tm", "firm", None),
        P("tm", "firm", None, None),
        P("tm", "firm"),
        P("tm", "firm"),
        P("firm", None),
        P("firm", None),
    ) + (P(),) * 9
    return jax.shard_map(body, mesh=mesh, in_specs=in_specs, out_specs=P("tm", "firm", None), check_vma=False)
```

```python
import math

import jax
import jax.numpy as jnp
from jax import lax
from jax.experimental import pallas as pl
from jax.experimental.pallas import tpu as pltpu
from jax.sharding import PartitionSpec as P

HEADS = 4
LAGS = 3
EARLY = 3
LATE = 5
SLOT = 16
LOG2 = math.log(2.0)
GELU = math.sqrt(2.0 / math.pi)
BF = jnp.bfloat16
F32 = jnp.float32
VM = pl.BlockSpec(memory_space=pltpu.VMEM)
SM = pl.BlockSpec(memory_space=pltpu.SMEM)
ANY = pl.BlockSpec(memory_space=pl.ANY)


def mm(a, b):
    return jnp.dot(a, b, preferred_element_type=F32)


def rms_norm(values, gain):
    scale = lax.rsqrt(jnp.mean(values * values, axis=-1, keepdims=True) + 1e-06)
    return values * scale * gain


def head_matrix(width):
    size = width // HEADS
    row = lax.broadcasted_iota(jnp.int32, (width, width), 0) // size
    col = lax.broadcasted_iota(jnp.int32, (width, width), 1) // size
    return jnp.where(row == col, 0.5 / math.sqrt(size), 0.0).astype(BF)


def attend(query, keys, values, head_sum):
    total = jnp.zeros(query.shape, F32)
    for key, value in zip(keys, values):
        value = value.astype(F32)
        total = total + (value + jnp.tanh(mm(query * key, head_sum) - LOG2) * value)
    return (0.5 * total).astype(BF)


def finish(mixed, attended, w_out, w_in, w_down, gain_ffn):
    second = mixed + mm(attended, w_out)
    normed2 = rms_norm(second, gain_ffn).astype(BF)
    x = mm(normed2, w_in)
    half = 0.5 * x
    inner = (half + half * jnp.tanh(x * (GELU + (GELU * 0.044715) * (x * x)))).astype(BF)
    return (second + mm(inner, w_down)).astype(BF)


def stack(parts):
    return jnp.concatenate(parts, axis=0)


def lagged(parts, count):
    return [stack(parts[LAGS - lag : LAGS - lag + count]) for lag in range(LAGS + 1)]


def own_kernel(where, counts, own, w_supply, base, tiles, scale):
    even = 2 - 2 * where[1]
    odd = 2 * where[1]
    for m in range(own.shape[0]):
        part = [counts[m, k].astype(F32) for k in range(3)]
        degree = 1.0 + jnp.sum(part[0] + part[1] + part[2], axis=-1, keepdims=True)
        inverse = lax.rsqrt(degree)
        feats = own[m]
        supplied = mm(feats, w_supply[...]).astype(BF)
        base[m] = feats.astype(F32) + inverse * mm(part[1].astype(BF), supplied)
        scale[m] = jnp.broadcast_to(inverse, scale.shape[1:])
        tiles[m, 0] = counts[m, even].astype(F32).astype(BF)
        tiles[m, 1] = counts[m, odd].astype(F32).astype(BF)


def mix(m, base, tiles, scale, even_rows, odd_rows, w_supply):
    message = mm(tiles[m, 0], mm(even_rows, w_supply).astype(BF))
    message = message + mm(tiles[m, 1], mm(odd_rows, w_supply).astype(BF))
    spread = jnp.concatenate([scale[m]] * (base.shape[-1] // scale.shape[-1]), axis=-1)
    return base + spread * message


def late_kernel(
    where, base, tiles, scale, even_rows, odd_rows, banks, sectors, *rest,
):
    tables, (w_supply, w_query, w_key, w_value, gain_mix) = rest[:4], rest[4:9]
    early_base, mixed_out, normed_out, query_out, key_out, value_out = rest[9:]
    me = where[0]
    rows_each, firms = tables[0].shape[0], base.shape[1]
    row = lax.broadcasted_iota(jnp.int32, (rows_each, firms), 0)
    normed = []
    for m in list(range(EARLY, EARLY + LATE)) + list(range(EARLY)):
        bank, sector = banks[m : m + 1], sectors[m : m + 1]
        bank = (lax.shift_right_logical(bank, 3) ^ me) * SLOT + (bank & 7)
        sector = (lax.shift_right_logical(sector, 2) ^ me) * SLOT + 8 + (sector & 3)
        total = base[m]
        for i, table in enumerate(tables):
            chosen = jnp.where((row == bank - i * rows_each) | (row == sector - i * rows_each), 1.0, 0.0)
            total = total + lax.dot_general(
                chosen.astype(BF), table[...], (((0,), (0,)), ((), ())), preferred_element_type=F32
            )
        if m < EARLY:
            early_base[m] = total
        else:
            i = m - EARLY
            mixed = mix(m, total, tiles, scale, even_rows[i], odd_rows[i], w_supply[...])
            mixed_out[i] = mixed
            normed.append(rms_norm(mixed, gain_mix[...]).astype(BF))
            if i >= LATE - LAGS:
                normed_out[i - LATE + LAGS] = normed[-1]
    shape = query_out.shape
    rows = stack(normed)
    query_out[...] = mm(rows, w_query[...]).astype(BF).reshape(shape)
    key_out[...] = mm(rows, w_key[...]).astype(BF).reshape(shape)
    value_out[...] = mm(rows, w_value[...]).astype(BF).reshape(shape)


def join_kernel(*refs):
    rows = refs[0].shape[0]
    for i, part in enumerate(refs[:-1]):
        refs[-1][i * rows : (i + 1) * rows] = part[...]


def write_back(final, buffer, result, sems, first):
    firms = buffer.shape[1]
    copies = []
    for i in range(buffer.shape[0]):
        buffer[i] = final[i * firms : (i + 1) * firms]
        copies.append(pltpu.make_async_copy(buffer.at[i], result.at[first + i], sems.at[i]))
        copies[-1].start()
    for copy in copies:
        copy.wait()


def last_kernel(mixed, query, key, value, w_out, w_in, w_down, gain_ffn, result, buffer, sems):
    count = LATE - LAGS
    firms, width = query.shape[1:]
    flat = (count * firms, width)
    keys = lagged([key[i] for i in range(LATE)], count)
    values = lagged([value[i] for i in range(LATE)], count)
    attended = attend(query[LAGS:].reshape(flat), keys, values, head_matrix(width))
    final = finish(mixed[LAGS:].reshape(flat), attended, w_out[...], w_in[...], w_down[...], gain_ffn[...])
    write_back(final, buffer, result, sems, EARLY + LAGS)


def early_kernel(
    base, tiles, scale, even_rows, odd_rows, late_mixed, late_query, late_key, late_value,
    w_supply, w_query, w_key, w_value, gain_mix, w_out, w_in, w_down, gain_ffn, started,
    result, mixed_out, query_out, key_out, value_out, buffer, sems,
):
    del started
    firms = base.shape[1]
    mixed, normed = [], []
    for m in range(EARLY):
        mixed.append(mix(m, base[m], tiles, scale, even_rows[m], odd_rows[m], w_supply[...]))
        normed.append(rms_norm(mixed[-1], gain_mix[...]).astype(BF))
    rows = stack(normed)
    cut = lambda rows: [rows[i * firms : (i + 1) * firms] for i in range(EARLY)]
    query = cut(mm(rows, w_query[...]).astype(BF))
    key = cut(mm(rows, w_key[...]).astype(BF))
    value = cut(mm(rows, w_value[...]).astype(BF))
    for m in range(LAGS):
        mixed_out[m], query_out[m], key_out[m], value_out[m] = mixed[m], query[m], key[m], value[m]
    keys = lagged(key + [late_key[m] for m in range(LAGS)], EARLY)
    values = lagged(value + [late_value[m] for m in range(LAGS)], EARLY)
    queries = stack(query[LAGS:] + [late_query[m] for m in range(LAGS)])
    attended = attend(queries, keys, values, head_matrix(base.shape[-1]))
    total = stack(mixed[LAGS:] + [late_mixed[m] for m in range(LAGS)])
    final = finish(total, attended, w_out[...], w_in[...], w_down[...], gain_ffn[...])
    write_back(final, buffer, result, sems, LAGS)


def first_kernel(
    earlier, mixed, query, key, value, w_key, w_value, w_out, w_in, w_down, gain_ffn, started, result, buffer, sems,
):
    del started
    firms, width = mixed.shape[1:]
    rows = earlier[...].reshape(LAGS * firms, width)
    cut = lambda rows: [rows[i * firms : (i + 1) * firms] for i in range(LAGS)]
    keys = lagged(cut(mm(rows, w_key[...]).astype(BF)) + [key[m] for m in range(LAGS)], LAGS)
    values = lagged(cut(mm(rows, w_value[...]).astype(BF)) + [value[m] for m in range(LAGS)], LAGS)
    flat = (LAGS * firms, width)
    attended = attend(query[...].reshape(flat), keys, values, head_matrix(width))
    final = finish(mixed[...].reshape(flat), attended, w_out[...], w_in[...], w_down[...], gain_ffn[...])
    write_back(final, buffer, result, sems, 0)


def body(
    features, supply_counts, bank_ids, sector_ids, bank_table, sector_table,
    w_supply, w_query, w_key, w_value, w_out, w_in, w_down, gain_mix, gain_ffn,
):
    months, firms, width = features.shape
    inner = w_in.shape[1]
    devices = lax.axis_size("firm")
    me = lax.axis_index("firm")
    where = jnp.stack([me, me & 1]).astype(jnp.int32)
    even_pairs = [(i, i ^ 1) for i in range(devices)]
    odd_pairs = [(i, i + 1) for i in range(1, devices - 1, 2)]
    odd_pairs = odd_pairs + [(j, i) for i, j in odd_pairs]

    def swap(x, bits):
        return lax.ppermute(x, "firm", [(i, i ^ bits) for i in range(devices)])

    spare = SLOT - bank_table.shape[0] - sector_table.shape[0]
    hub = jnp.concatenate([bank_table, sector_table, jnp.zeros((spare, width), BF)], axis=0)
    near = [hub] + [swap(hub, i) for i in (1, 2, 3)]
    late = features[EARLY:]
    late_even = lax.ppermute(late, "firm", even_pairs)
    late_odd = lax.ppermute(late, "firm", odd_pairs)

    def joined(parts):
        rows = parts[0].shape[0]
        return pl.pallas_call(
            join_kernel,
            in_specs=[VM] * len(parts),
            out_specs=VM,
            out_shape=jax.ShapeDtypeStruct((len(parts) * rows, width), BF),
            cost_estimate=pl.CostEstimate(flops=0, bytes_accessed=1 << 10, transcendentals=0),
            name="join",
        )(*parts)

    def spread(near):
        hub = joined(near)
        hub = joined([hub] + [swap(hub, i) for i in (4, 8, 12)])
        return [hub] + [swap(hub, i) for i in (16, 32, 48)]

    tables = spread(near)
    tables, early = lax.optimization_barrier((tables, features[:EARLY]))
    early_even = lax.ppermute(early, "firm", even_pairs)
    early_odd = lax.ppermute(early, "firm", odd_pairs)

    counts = jnp.transpose(supply_counts, (0, 2, 1, 3))
    gain_mix = gain_mix.reshape(1, width)
    gain_ffn = gain_ffn.reshape(1, width)

    def cost(units, kibibytes):
        return pl.CostEstimate(
            flops=2 * units * firms * width * width, bytes_accessed=kibibytes << 10, transcendentals=0
        )

    def like(count, dtype, lanes=width):
        return jax.ShapeDtypeStruct((count, firms, lanes), dtype)

    params = pltpu.CompilerParams(vmem_limit_bytes=28 << 20)
    step = lambda *shape: pl.BlockSpec((2,) + shape, lambda m: (m,) + (0,) * len(shape))
    base, tiles, scale = pl.pallas_call(
        own_kernel,
        grid=(months // 2,),
        in_specs=[
            SM, step(3, firms, firms), step(firms, width), pl.BlockSpec((width, width), lambda m: (0, 0)),
        ],
        out_specs=[step(firms, width), step(2, firms, firms), step(firms, 128)],
        out_shape=[
            like(months, F32), jax.ShapeDtypeStruct((months, 2, firms, firms), BF), like(months, F32, 128),
        ],
        compiler_params=params,
        cost_estimate=cost(200, 1 << 14),
        name="own_block",
    )(where, counts, features, w_supply)

    early_base, late_mixed, late_normed, late_query, late_key, late_value = pl.pallas_call(
        late_kernel,
        in_specs=[SM] + [VM] * 16,
        out_specs=[VM] * 6,
        out_shape=[
            like(EARLY, F32), like(LATE, F32), like(LAGS, BF), like(LATE, BF), like(LATE, BF), like(LATE, BF),
        ],
        compiler_params=params,
        cost_estimate=cost(1, 1),
        name="late_months",
    )(
        where, base, tiles, scale, late_even, late_odd, bank_ids, sector_ids, *tables,
        w_supply, w_query, w_key, w_value, gain_mix,
    )

    earlier = lax.ppermute(late_normed, "tm", [(i, i + 1) for i in range(lax.axis_size("tm") - 1)])
    end_weights = (w_out, w_in, w_down, gain_ffn)

    def scratch(count):
        return [pltpu.VMEM((count, firms, width), BF), pltpu.SemaphoreType.DMA((count,))]

    result = pl.pallas_call(
        last_kernel,
        in_specs=[VM] * 8,
        out_specs=ANY,
        out_shape=like(months, BF),
        scratch_shapes=scratch(LATE - LAGS),
        compiler_params=params,
        cost_estimate=cost(1, 1),
        name="last_month",
    )(late_mixed, late_query, late_key, late_value, *end_weights)

    result, mixed, query, key, value = pl.pallas_call(
        early_kernel,
        in_specs=[VM] * 18 + [ANY],
        out_specs=[ANY] + [VM] * 4,
        out_shape=[like(months, BF), like(LAGS, F32), like(LAGS, BF), like(LAGS, BF), like(LAGS, BF)],
        scratch_shapes=scratch(EARLY),
        input_output_aliases={18: 0},
        compiler_params=params,
        cost_estimate=cost(1, 1),
        name="early_months",
    )(
        early_base, tiles, scale, early_even, early_odd, late_mixed, late_query, late_key, late_value,
        w_supply, w_query, w_key, w_value, gain_mix, *end_weights, result,
    )

    return pl.pallas_call(
        first_kernel,
        in_specs=[VM] * 11 + [ANY],
        out_specs=ANY,
        out_shape=like(months, BF),
        scratch_shapes=scratch(LAGS),
        input_output_aliases={11: 0},
        compiler_params=params,
        cost_estimate=cost(1, 1),
        name="first_months",
    )(earlier, mixed, query, key, value, w_key, w_value, *end_weights, result)


def solution(mesh):
    in_specs = (
        P("tm", "firm", None),
        P("tm", "firm", None, None),
        P("tm", "firm"),
        P("tm", "firm"),
        P("firm", None),
        P("firm", None),
    ) + (P(),) * 9
    return jax.shard_map(body, mesh=mesh, in_specs=in_specs, out_specs=P("tm", "firm", None), check_vma=False)
```

```python
import math

import jax
import jax.numpy as jnp
from jax import lax
from jax.experimental import pallas as pl
from jax.experimental.pallas import tpu as pltpu
from jax.sharding import PartitionSpec as P

HEADS = 4
LAGS = 3
EARLY = 3
LATE = 5
SLOT = 16
LOG2 = math.log(2.0)
GELU = math.sqrt(2.0 / math.pi)
BF = jnp.bfloat16
F32 = jnp.float32
VM = pl.BlockSpec(memory_space=pltpu.VMEM)
SM = pl.BlockSpec(memory_space=pltpu.SMEM)
ANY = pl.BlockSpec(memory_space=pl.ANY)


def mm(a, b):
    return jnp.dot(a, b, preferred_element_type=F32)


def rms_norm(values, gain):
    scale = lax.rsqrt(jnp.mean(values * values, axis=-1, keepdims=True) + 1e-06)
    return values * scale * gain


def head_matrix(width):
    size = width // HEADS
    row = lax.broadcasted_iota(jnp.int32, (width, width), 0) // size
    col = lax.broadcasted_iota(jnp.int32, (width, width), 1) // size
    return jnp.where(row == col, 0.5 / math.sqrt(size), 0.0).astype(BF)


def attend(query, keys, values, head_sum):
    total = jnp.zeros(query.shape, F32)
    for key, value in zip(keys, values):
        value = value.astype(F32)
        total = total + (value + jnp.tanh(mm(query * key, head_sum) - LOG2) * value)
    return (0.5 * total).astype(BF)


def finish(mixed, attended, w_out, w_in, w_down, gain_ffn):
    second = mixed + mm(attended, w_out)
    normed2 = rms_norm(second, gain_ffn).astype(BF)
    x = mm(normed2, w_in)
    half = 0.5 * x
    inner = (half + half * jnp.tanh(x * (GELU + (GELU * 0.044715) * (x * x)))).astype(BF)
    return (second + mm(inner, w_down)).astype(BF)


def stack(parts):
    return jnp.concatenate(parts, axis=0)


def lagged(parts, count):
    return [stack(parts[LAGS - lag : LAGS - lag + count]) for lag in range(LAGS + 1)]


def own_kernel(where, counts, own, w_supply, base, tiles, scale):
    even = 2 - 2 * where[1]
    odd = 2 * where[1]
    for m in range(own.shape[0]):
        part = [counts[m, k].astype(F32) for k in range(3)]
        degree = 1.0 + jnp.sum(part[0] + part[1] + part[2], axis=-1, keepdims=True)
        inverse = lax.rsqrt(degree)
        feats = own[m]
        supplied = mm(feats, w_supply[...]).astype(BF)
        base[m] = feats.astype(F32) + inverse * mm(part[1].astype(BF), supplied)
        scale[m] = jnp.broadcast_to(inverse, scale.shape[1:])
        tiles[m, 0] = counts[m, even].astype(F32).astype(BF)
        tiles[m, 1] = counts[m, odd].astype(F32).astype(BF)


def mix(m, base, tiles, scale, even_rows, odd_rows, w_supply):
    message = mm(tiles[m, 0], mm(even_rows, w_supply).astype(BF))
    message = message + mm(tiles[m, 1], mm(odd_rows, w_supply).astype(BF))
    spread = jnp.concatenate([scale[m]] * (base.shape[-1] // scale.shape[-1]), axis=-1)
    return base + spread * message


def slot(apart):
    return apart ^ ((apart & 21) << 1)


def late_kernel(
    where, base, tiles, scale, odd_rows, even_rows, banks, sectors, *rest,
):
    tables, (w_supply, w_query, w_key, w_value, gain_mix) = rest[:4], rest[4:9]
    early_base, mixed_out, normed_out, query_out, key_out, value_out = rest[9:]
    me = where[0]
    rows_each, firms = tables[0].shape[0], base.shape[1]
    row = lax.broadcasted_iota(jnp.int32, (rows_each, firms), 0)
    normed = []
    for m in list(range(EARLY, EARLY + LATE)) + list(range(EARLY)):
        bank, sector = banks[m : m + 1], sectors[m : m + 1]
        bank = slot(lax.shift_right_logical(bank, 3) ^ me) * SLOT + (bank & 7)
        sector = slot(lax.shift_right_logical(sector, 2) ^ me) * SLOT + 8 + (sector & 3)
        total = base[m]
        for i, table in enumerate(tables):
            chosen = jnp.where((row == bank - i * rows_each) | (row == sector - i * rows_each), 1.0, 0.0)
            total = total + lax.dot_general(
                chosen.astype(BF), table[...], (((0,), (0,)), ((), ())), preferred_element_type=F32
            )
        if m < EARLY:
            early_base[m] = total
        else:
            i = m - EARLY
            mixed = mix(m, total, tiles, scale, even_rows[i], odd_rows[i], w_supply[...])
            mixed_out[i] = mixed
            normed.append(rms_norm(mixed, gain_mix[...]).astype(BF))
            if i >= LATE - LAGS:
                normed_out[i - LATE + LAGS] = normed[-1]
    shape = query_out.shape
    rows = stack(normed)
    query_out[...] = mm(rows, w_query[...]).astype(BF).reshape(shape)
    key_out[...] = mm(rows, w_key[...]).astype(BF).reshape(shape)
    value_out[...] = mm(rows, w_value[...]).astype(BF).reshape(shape)


def join_kernel(*refs):
    rows = refs[0].shape[0]
    for i, part in enumerate(refs[:-1]):
        refs[-1][i * rows : (i + 1) * rows] = part[...]


def write_back(final, buffer, result, sems, first):
    firms = buffer.shape[1]
    copies = []
    for i in range(buffer.shape[0]):
        buffer[i] = final[i * firms : (i + 1) * firms]
        copies.append(pltpu.make_async_copy(buffer.at[i], result.at[first + i], sems.at[i]))
        copies[-1].start()
    for copy in copies:
        copy.wait()


def last_kernel(mixed, query, key, value, w_out, w_in, w_down, gain_ffn, result, buffer, sems):
    count = LATE - LAGS
    firms, width = query.shape[1:]
    flat = (count * firms, width)
    keys = lagged([key[i] for i in range(LATE)], count)
    values = lagged([value[i] for i in range(LATE)], count)
    attended = attend(query[LAGS:].reshape(flat), keys, values, head_matrix(width))
    final = finish(mixed[LAGS:].reshape(flat), attended, w_out[...], w_in[...], w_down[...], gain_ffn[...])
    write_back(final, buffer, result, sems, EARLY + LAGS)


def early_kernel(
    earlier, base, tiles, scale, odd_rows, even_rows, late_mixed, late_query, late_key, late_value,
    w_supply, w_query, w_key, w_value, gain_mix, w_out, w_in, w_down, gain_ffn, started,
    result, buffer, sems,
):
    del started
    firms, width = base.shape[1:]
    heads = head_matrix(width)
    cut = lambda rows: [rows[i * firms : (i + 1) * firms] for i in range(rows.shape[0] // firms)]
    mixed, normed = [], []
    for m in range(EARLY):
        mixed.append(mix(m, base[m], tiles, scale, even_rows[m], odd_rows[m], w_supply[...]))
        normed.append(rms_norm(mixed[-1], gain_mix[...]).astype(BF))
    query = cut(mm(stack(normed), w_query[...]).astype(BF)) + [late_query[m] for m in range(LAGS)]
    rows = stack([earlier[...].reshape(LAGS * firms, width)] + normed)
    key = cut(mm(rows, w_key[...]).astype(BF)) + [late_key[m] for m in range(LAGS)]
    value = cut(mm(rows, w_value[...]).astype(BF)) + [late_value[m] for m in range(LAGS)]
    mixed = mixed + [late_mixed[m] for m in range(LAGS)]
    copies = []
    for first in range(0, EARLY + LAGS, LAGS):
        months = slice(first, first + LAGS)
        keys = lagged(key[first : first + 2 * LAGS], LAGS)
        values = lagged(value[first : first + 2 * LAGS], LAGS)
        attended = attend(stack(query[months]), keys, values, heads)
        final = finish(stack(mixed[months]), attended, w_out[...], w_in[...], w_down[...], gain_ffn[...])
        buffer[months] = final.reshape(LAGS, firms, width)
        copies.append(pltpu.make_async_copy(buffer.at[months], result.at[months], sems.at[first // LAGS]))
        copies[-1].start()
    for copy in copies:
        copy.wait()


def body(
    features, supply_counts, bank_ids, sector_ids, bank_table, sector_table,
    w_supply, w_query, w_key, w_value, w_out, w_in, w_down, gain_mix, gain_ffn,
):
    months, firms, width = features.shape
    inner = w_in.shape[1]
    devices = lax.axis_size("firm")
    me = lax.axis_index("firm")
    where = jnp.stack([me, me & 1]).astype(jnp.int32)
    even_pairs = [(i, i ^ 1) for i in range(devices)]
    odd_pairs = [(i, i + 1) for i in range(1, devices - 1, 2)]
    odd_pairs = odd_pairs + [(j, i) for i, j in odd_pairs]

    def swap(x, bits):
        return lax.ppermute(x, "firm", [(i, i ^ bits) for i in range(devices)])

    spare = SLOT - bank_table.shape[0] - sector_table.shape[0]
    hub = jnp.concatenate([bank_table, sector_table, jnp.zeros((spare, width), BF)], axis=0)
    near = [hub] + [swap(hub, i) for i in (3, 2, 1)]
    late = features[EARLY:]
    late_even = lax.ppermute(late, "firm", even_pairs)
    late_odd = lax.ppermute(late, "firm", odd_pairs)

    def joined(parts):
        rows = parts[0].shape[0]
        return pl.pallas_call(
            join_kernel,
            in_specs=[VM] * len(parts),
            out_specs=VM,
            out_shape=jax.ShapeDtypeStruct((len(parts) * rows, width), BF),
            cost_estimate=pl.CostEstimate(flops=0, bytes_accessed=1 << 10, transcendentals=0),
            name="join",
        )(*parts)

    def spread(near):
        hub = joined(near)
        hub = joined([hub] + [swap(hub, i) for i in (12, 8, 4)])
        return [hub] + [swap(hub, i) for i in (48, 32, 16)]

    tables = spread(near)
    tables, early = lax.optimization_barrier((tables, features[:EARLY]))
    early_even = lax.ppermute(early, "firm", even_pairs)
    early_odd = lax.ppermute(early, "firm", odd_pairs)

    counts = jnp.transpose(supply_counts, (0, 2, 1, 3))
    gain_mix = gain_mix.reshape(1, width)
    gain_ffn = gain_ffn.reshape(1, width)

    def cost(units, kibibytes):
        return pl.CostEstimate(
            flops=2 * units * firms * width * width, bytes_accessed=kibibytes << 10, transcendentals=0
        )

    def like(count, dtype, lanes=width):
        return jax.ShapeDtypeStruct((count, firms, lanes), dtype)

    params = pltpu.CompilerParams(vmem_limit_bytes=28 << 20)
    step = lambda *shape: pl.BlockSpec((2,) + shape, lambda m: (m,) + (0,) * len(shape))
    base, tiles, scale = pl.pallas_call(
        own_kernel,
        grid=(months // 2,),
        in_specs=[
            SM, step(3, firms, firms), step(firms, width), pl.BlockSpec((width, width), lambda m: (0, 0)),
        ],
        out_specs=[step(firms, width), step(2, firms, firms), step(firms, 128)],
        out_shape=[
            like(months, F32), jax.ShapeDtypeStruct((months, 2, firms, firms), BF), like(months, F32, 128),
        ],
        compiler_params=params,
        cost_estimate=cost(200, 1 << 14),
        name="own_block",
    )(where, counts, features, w_supply)

    early_base, late_mixed, late_normed, late_query, late_key, late_value = pl.pallas_call(
        late_kernel,
        in_specs=[SM] + [VM] * 16,
        out_specs=[VM] * 6,
        out_shape=[
            like(EARLY, F32), like(LATE, F32), like(LAGS, BF), like(LATE, BF), like(LATE, BF), like(LATE, BF),
        ],
        compiler_params=params,
        cost_estimate=cost(1, 1),
        name="late_months",
    )(
        where, base, tiles, scale, late_odd, late_even, bank_ids, sector_ids, *tables,
        w_supply, w_query, w_key, w_value, gain_mix,
    )

    earlier = lax.ppermute(late_normed, "tm", [(i, i + 1) for i in range(lax.axis_size("tm") - 1)])
    end_weights = (w_out, w_in, w_down, gain_ffn)

    def scratch(count):
        return [pltpu.VMEM((count, firms, width), BF), pltpu.SemaphoreType.DMA((count,))]

    result = pl.pallas_call(
        last_kernel,
        in_specs=[VM] * 8,
        out_specs=ANY,
        out_shape=like(months, BF),
        scratch_shapes=scratch(LATE - LAGS),
        compiler_params=params,
        cost_estimate=cost(1, 1),
        name="last_month",
    )(late_mixed, late_query, late_key, late_value, *end_weights)

    return pl.pallas_call(
        early_kernel,
        in_specs=[VM] * 19 + [ANY],
        out_specs=ANY,
        out_shape=like(months, BF),
        scratch_shapes=[pltpu.VMEM((EARLY + LAGS, firms, width), BF), pltpu.SemaphoreType.DMA((2,))],
        input_output_aliases={19: 0},
        compiler_params=params,
        cost_estimate=cost(1, 1),
        name="early_months",
    )(
        earlier, early_base, tiles, scale, early_odd, early_even, late_mixed, late_query, late_key, late_value,
        w_supply, w_query, w_key, w_value, gain_mix, *end_weights, result,
    )


def solution(mesh):
    in_specs = (
        P("tm", "firm", None),
        P("tm", "firm", None, None),
        P("tm", "firm"),
        P("tm", "firm"),
        P("firm", None),
        P("firm", None),
    ) + (P(),) * 9
    return jax.shard_map(body, mesh=mesh, in_specs=in_specs, out_specs=P("tm", "firm", None), check_vma=False)
```

```python
import math

import jax
import jax.numpy as jnp
from jax import lax
from jax.experimental import pallas as pl
from jax.experimental.pallas import tpu as pltpu
from jax.sharding import PartitionSpec as P

HEADS = 4
LAGS = 3
EARLY = 3
LATE = 5
SLOT = 16
LOG2 = math.log(2.0)
GELU = math.sqrt(2.0 / math.pi)
BF = jnp.bfloat16
F32 = jnp.float32
VM = pl.BlockSpec(memory_space=pltpu.VMEM)
SM = pl.BlockSpec(memory_space=pltpu.SMEM)
ANY = pl.BlockSpec(memory_space=pl.ANY)


def mm(a, b):
    return jnp.dot(a, b, preferred_element_type=F32)


def rms_norm(values, gain):
    scale = lax.rsqrt(jnp.mean(values * values, axis=-1, keepdims=True) + 1e-06)
    return values * scale * gain


def head_matrix(width):
    size = width // HEADS
    row = lax.broadcasted_iota(jnp.int32, (width, width), 0) // size
    col = lax.broadcasted_iota(jnp.int32, (width, width), 1) // size
    return jnp.where(row == col, 0.5 / math.sqrt(size), 0.0).astype(BF)


def attend(query, keys, values, head_sum):
    total = jnp.zeros(query.shape, F32)
    for key, value in zip(keys, values):
        value = value.astype(F32)
        total = total + (value + jnp.tanh(mm(query * key, head_sum) - LOG2) * value)
    return (0.5 * total).astype(BF)


def finish(mixed, attended, w_out, w_in, w_down, gain_ffn):
    second = mixed + mm(attended, w_out)
    normed2 = rms_norm(second, gain_ffn).astype(BF)
    x = mm(normed2, w_in)
    half = 0.5 * x
    inner = (half + half * jnp.tanh(x * (GELU + (GELU * 0.044715) * (x * x)))).astype(BF)
    return (second + mm(inner, w_down)).astype(BF)


def stack(parts):
    return jnp.concatenate(parts, axis=0)


def lagged(parts, count):
    return [stack(parts[LAGS - lag : LAGS - lag + count]) for lag in range(LAGS + 1)]


def own_kernel(where, counts, own, w_supply, base, tiles, scale):
    even = 2 - 2 * where[1]
    odd = 2 * where[1]
    for m in range(own.shape[0]):
        part = [counts[m, k].astype(F32) for k in range(3)]
        degree = 1.0 + jnp.sum(part[0] + part[1] + part[2], axis=-1, keepdims=True)
        inverse = lax.rsqrt(degree)
        feats = own[m]
        supplied = mm(feats, w_supply[...]).astype(BF)
        base[m] = feats.astype(F32) + inverse * mm(part[1].astype(BF), supplied)
        scale[m] = jnp.broadcast_to(inverse, scale.shape[1:])
        tiles[m, 0] = counts[m, even].astype(F32).astype(BF)
        tiles[m, 1] = counts[m, odd].astype(F32).astype(BF)


def mix(m, base, tiles, scale, even_rows, odd_rows, w_supply):
    message = mm(tiles[m, 0], mm(even_rows, w_supply).astype(BF))
    message = message + mm(tiles[m, 1], mm(odd_rows, w_supply).astype(BF))
    spread = jnp.concatenate([scale[m]] * (base.shape[-1] // scale.shape[-1]), axis=-1)
    return base + spread * message


def slot(apart):
    return apart ^ ((apart & 21) << 1)


def with_hubs(m, me, base, banks, sectors, tables):
    rows_each, firms = tables[0].shape[0], base.shape[1]
    row = lax.broadcasted_iota(jnp.int32, (rows_each, firms), 0)
    bank, sector = banks[m : m + 1], sectors[m : m + 1]
    bank = slot(lax.shift_right_logical(bank, 3) ^ me) * SLOT + (bank & 7)
    sector = slot(lax.shift_right_logical(sector, 2) ^ me) * SLOT + 8 + (sector & 3)
    total = base[m]
    for i, table in enumerate(tables):
        chosen = jnp.where((row == bank - i * rows_each) | (row == sector - i * rows_each), 1.0, 0.0)
        total = total + lax.dot_general(
            chosen.astype(BF), table[...], (((0,), (0,)), ((), ())), preferred_element_type=F32
        )
    return total


def late_kernel(
    where, base, tiles, scale, odd_rows, even_rows, banks, sectors, *rest,
):
    tables, (w_supply, w_query, w_key, w_value, gain_mix) = rest[:4], rest[4:9]
    mixed_out, normed_out, query_out, key_out, value_out = rest[9:]
    firms = base.shape[1]
    normed = []
    for i in range(LATE):
        m = EARLY + i
        total = with_hubs(m, where[0], base, banks, sectors, tables)
        mixed = mix(m, total, tiles, scale, even_rows[i], odd_rows[i], w_supply[...])
        mixed_out[i] = mixed
        normed.append(rms_norm(mixed, gain_mix[...]).astype(BF))
        if i >= LATE - LAGS:
            normed_out[i - LATE + LAGS] = normed[-1]
    shape = query_out.shape
    rows = stack(normed)
    query_out[...] = mm(rows, w_query[...]).astype(BF).reshape(shape)
    key_out[...] = mm(rows, w_key[...]).astype(BF).reshape(shape)
    value_out[...] = mm(rows, w_value[...]).astype(BF).reshape(shape)


def join_kernel(*refs):
    rows = refs[0].shape[0]
    for i, part in enumerate(refs[:-1]):
        refs[-1][i * rows : (i + 1) * rows] = part[...]


def write_back(final, buffer, result, sems, first):
    firms = buffer.shape[1]
    copies = []
    for i in range(buffer.shape[0]):
        buffer[i] = final[i * firms : (i + 1) * firms]
        copies.append(pltpu.make_async_copy(buffer.at[i], result.at[first + i], sems.at[i]))
        copies[-1].start()
    for copy in copies:
        copy.wait()


def last_kernel(
    where, base, banks, sectors, *rest,
):
    tables, (mixed, query, key, value, w_out, w_in, w_down, gain_ffn) = rest[:4], rest[4:12]
    result, early_base, buffer, sems = rest[12:]
    for m in range(EARLY):
        early_base[m] = with_hubs(m, where[0], base, banks, sectors, tables)
    count = LATE - LAGS
    firms, width = query.shape[1:]
    flat = (count * firms, width)
    keys = lagged([key[i] for i in range(LATE)], count)
    values = lagged([value[i] for i in range(LATE)], count)
    attended = attend(query[LAGS:].reshape(flat), keys, values, head_matrix(width))
    final = finish(mixed[LAGS:].reshape(flat), attended, w_out[...], w_in[...], w_down[...], gain_ffn[...])
    write_back(final, buffer, result, sems, EARLY + LAGS)


def early_kernel(
    earlier, base, tiles, scale, odd_rows, even_rows, late_mixed, late_query, late_key, late_value,
    w_supply, w_query, w_key, w_value, gain_mix, w_out, w_in, w_down, gain_ffn, started,
    result, buffer, sems,
):
    del started
    firms, width = base.shape[1:]
    heads = head_matrix(width)
    cut = lambda rows: [rows[i * firms : (i + 1) * firms] for i in range(rows.shape[0] // firms)]
    mixed, normed = [], []
    for m in range(EARLY):
        mixed.append(mix(m, base[m], tiles, scale, even_rows[m], odd_rows[m], w_supply[...]))
        normed.append(rms_norm(mixed[-1], gain_mix[...]).astype(BF))
    query = cut(mm(stack(normed), w_query[...]).astype(BF)) + [late_query[m] for m in range(LAGS)]
    rows = stack([earlier[...].reshape(LAGS * firms, width)] + normed)
    key = cut(mm(rows, w_key[...]).astype(BF)) + [late_key[m] for m in range(LAGS)]
    value = cut(mm(rows, w_value[...]).astype(BF)) + [late_value[m] for m in range(LAGS)]
    mixed = mixed + [late_mixed[m] for m in range(LAGS)]
    copies = []
    for first in range(0, EARLY + LAGS, LAGS):
        months = slice(first, first + LAGS)
        keys = lagged(key[first : first + 2 * LAGS], LAGS)
        values = lagged(value[first : first + 2 * LAGS], LAGS)
        attended = attend(stack(query[months]), keys, values, heads)
        final = finish(stack(mixed[months]), attended, w_out[...], w_in[...], w_down[...], gain_ffn[...])
        buffer[months] = final.reshape(LAGS, firms, width)
        copies.append(pltpu.make_async_copy(buffer.at[months], result.at[months], sems.at[first // LAGS]))
        copies[-1].start()
    for copy in copies:
        copy.wait()


def body(
    features, supply_counts, bank_ids, sector_ids, bank_table, sector_table,
    w_supply, w_query, w_key, w_value, w_out, w_in, w_down, gain_mix, gain_ffn,
):
    months, firms, width = features.shape
    inner = w_in.shape[1]
    devices = lax.axis_size("firm")
    me = lax.axis_index("firm")
    where = jnp.stack([me, me & 1]).astype(jnp.int32)
    even_pairs = [(i, i ^ 1) for i in range(devices)]
    odd_pairs = [(i, i + 1) for i in range(1, devices - 1, 2)]
    odd_pairs = odd_pairs + [(j, i) for i, j in odd_pairs]

    def swap(x, bits):
        return lax.ppermute(x, "firm", [(i, i ^ bits) for i in range(devices)])

    spare = SLOT - bank_table.shape[0] - sector_table.shape[0]
    hub = jnp.concatenate([bank_table, sector_table, jnp.zeros((spare, width), BF)], axis=0)
    near = [hub] + [swap(hub, i) for i in (3, 2, 1)]
    late = features[EARLY:]
    late_even = lax.ppermute(late, "firm", even_pairs)
    late_odd = lax.ppermute(late, "firm", odd_pairs)

    def joined(parts):
        rows = parts[0].shape[0]
        return pl.pallas_call(
            join_kernel,
            in_specs=[VM] * len(parts),
            out_specs=VM,
            out_shape=jax.ShapeDtypeStruct((len(parts) * rows, width), BF),
            cost_estimate=pl.CostEstimate(flops=0, bytes_accessed=1 << 10, transcendentals=0),
            name="join",
        )(*parts)

    def spread(near):
        hub = joined(near)
        hub = joined([hub] + [swap(hub, i) for i in (12, 8, 4)])
        return [hub] + [swap(hub, i) for i in (48, 32, 16)]

    tables = spread(near)
    tables, early = lax.optimization_barrier((tables, features[:EARLY]))
    early_even = lax.ppermute(early, "firm", even_pairs)
    early_odd = lax.ppermute(early, "firm", odd_pairs)

    counts = jnp.transpose(supply_counts, (0, 2, 1, 3))
    gain_mix = gain_mix.reshape(1, width)
    gain_ffn = gain_ffn.reshape(1, width)

    def cost(units, kibibytes):
        return pl.CostEstimate(
            flops=2 * units * firms * width * width, bytes_accessed=kibibytes << 10, transcendentals=0
        )

    def like(count, dtype, lanes=width):
        return jax.ShapeDtypeStruct((count, firms, lanes), dtype)

    params = pltpu.CompilerParams(vmem_limit_bytes=28 << 20)
    step = lambda *shape: pl.BlockSpec((2,) + shape, lambda m: (m,) + (0,) * len(shape))
    base, tiles, scale = pl.pallas_call(
        own_kernel,
        grid=(months // 2,),
        in_specs=[
            SM, step(3, firms, firms), step(firms, width), pl.BlockSpec((width, width), lambda m: (0, 0)),
        ],
        out_specs=[step(firms, width), step(2, firms, firms), step(firms, 128)],
        out_shape=[
            like(months, F32), jax.ShapeDtypeStruct((months, 2, firms, firms), BF), like(months, F32, 128),
        ],
        compiler_params=params,
        cost_estimate=cost(200, 1 << 14),
        name="own_block",
    )(where, counts, features, w_supply)

    late_mixed, late_normed, late_query, late_key, late_value = pl.pallas_call(
        late_kernel,
        in_specs=[SM] + [VM] * 16,
        out_specs=[VM] * 5,
        out_shape=[
            like(LATE, F32), like(LAGS, BF), like(LATE, BF), like(LATE, BF), like(LATE, BF),
        ],
        compiler_params=params,
        cost_estimate=cost(1, 1),
        name="late_months",
    )(
        where, base, tiles, scale, late_odd, late_even, bank_ids, sector_ids, *tables,
        w_supply, w_query, w_key, w_value, gain_mix,
    )

    earlier = lax.ppermute(late_normed, "tm", [(i, i + 1) for i in range(lax.axis_size("tm") - 1)])
    end_weights = (w_out, w_in, w_down, gain_ffn)

    def scratch(count):
        return [pltpu.VMEM((count, firms, width), BF), pltpu.SemaphoreType.DMA((count,))]

    result, early_base = pl.pallas_call(
        last_kernel,
        in_specs=[SM] + [VM] * 15,
        out_specs=[ANY, VM],
        out_shape=[like(months, BF), like(EARLY, F32)],
        scratch_shapes=scratch(LATE - LAGS),
        compiler_params=params,
        cost_estimate=cost(1, 1),
        name="last_month",
    )(
        where, base, bank_ids, sector_ids, *tables, late_mixed, late_query, late_key, late_value, *end_weights,
    )

    return pl.pallas_call(
        early_kernel,
        in_specs=[VM] * 19 + [ANY],
        out_specs=ANY,
        out_shape=like(months, BF),
        scratch_shapes=[pltpu.VMEM((EARLY + LAGS, firms, width), BF), pltpu.SemaphoreType.DMA((2,))],
        input_output_aliases={19: 0},
        compiler_params=params,
        cost_estimate=cost(1, 1),
        name="early_months",
    )(
        earlier, early_base, tiles, scale, early_odd, early_even, late_mixed, late_query, late_key, late_value,
        w_supply, w_query, w_key, w_value, gain_mix, *end_weights, result,
    )


def solution(mesh):
    in_specs = (
        P("tm", "firm", None),
        P("tm", "firm", None, None),
        P("tm", "firm"),
        P("tm", "firm"),
        P("firm", None),
        P("firm", None),
    ) + (P(),) * 9
    return jax.shard_map(body, mesh=mesh, in_specs=in_specs, out_specs=P("tm", "firm", None), check_vma=False)
```
